32 devices in a mesh: sims: 4 (over x, core), blk: 8 (over z, y).
Axes of the slice: x: 2, y: 2, z: 4, core: 2. Of those that a mesh axis runs over, the one named last changes fastest.
Arguments:
- sim_alm: bfloat16 [1536, 16, 2, 1536], P('blk', 'sims'), may hold values from -6 to 6
- t_filter: float32 [1536], replicated, may hold values from 0.0006510417 to 0.00390625
- wiener_filter: float32 [1536], replicated, may hold values from 8.477105e-07 to 5.086263e-06
- colatitude: float32 [16], replicated, may hold values from 1.18672 to 1.51328, as said below
- legendre: bfloat16 [1536, 1536, 16], P('blk'), may hold values from -2 to 2, as said below
- pixel_mask: int32 [16, 4096], P('blk'), may hold values 0 or 1
Outputs:
- field_sum: float32 [1536, 2, 1536], P('blk', None, 'sims')
- spectra: float32 [16, 2, 1536], P('sims')
The draws below stay inside these ranges and needn't reach their ends.
Inputs may be any that keep to these rules, and one draw needn't show every extreme that they name: `colatitude`: the colatitudes of 16 cycles in increasing order, about 0.0016 apart, in a band centred between 1.2 and 1.5. legendre[m,l,r] is the orthonormal associated Legendre function of degree l and order m at colatitude[r], zero for l < m, rounded to bfloat16.
All inputs are finite; a program needn't handle non-finite values. No bound on the sum of `pixel_mask` on one device may be relied on, other than what follows from the above.
Results may differ from the reference program's by a relative error of at most 0.006.
The reference program's roundings to bfloat16 on the way (of `coefs`, `cycle_coefs`, `fourier`, `flow_maps`, `mode_coefs` and `tilted`) count: a program that leaves them out, or rounds other values in their place, can miss the bound.
Values may be sent and summed in bfloat16 or wider, within the bound.
A program may use at most 192 MiB of HBM per device.

```python
import math
import jax
import jax.numpy as jnp
from jax import lax

L = 1536
NPHI = 4096
CYCLES = 16
NSIM = 16


def cycle_angles(key):
    jitter = jax.random.uniform(jax.random.fold_in(key, 11), (CYCLES,), jnp.float32, -0.3, 0.3)
    center = jax.random.uniform(jax.random.fold_in(key, 17), (), jnp.float32, 1.2, 1.5)
    spacing = jnp.arange(CYCLES, dtype=jnp.float32) + 0.5 - CYCLES / 2.0 + jitter
    return center + 0.0016 * spacing


def draw_colatitude(key, part):
    return cycle_angles(key)


def draw_legendre(key, part):
    angles = cycle_angles(key)
    cosine = jnp.cos(angles)[None, :]
    log_sine = jnp.log(jnp.sin(angles))[None, :]
    orders = jnp.arange(L, dtype=jnp.float32)[:, None]
    counting = jnp.arange(1, L, dtype=jnp.float32)
    halves = jnp.log((2.0 * counting - 1.0) / (2.0 * counting))
    running = jnp.concatenate([jnp.zeros((1,), jnp.float32), jnp.cumsum(halves)])[:, None]
    diagonal = jnp.exp(0.5 * jnp.log((2.0 * orders + 1.0) / (4.0 * math.pi)) + 0.5 * running + orders * log_sine)

    def advance(state_pair, degree):
        previous, older = state_pair
        ratio_now = jnp.sqrt(jnp.maximum(4.0 * degree * degree - 1.0, 1.0) / jnp.maximum(degree * degree - orders * orders, 1.0))
        lower_degree = degree - 1.0
        ratio_before = jnp.sqrt(jnp.maximum(4.0 * lower_degree * lower_degree - 1.0, 1.0) / jnp.maximum(lower_degree * lower_degree - orders * orders, 1.0))
        general = ratio_now * (cosine * previous - older / ratio_before)
        current = jnp.where(degree == orders, diagonal, jnp.where(degree > orders, general, 0.0))
        return ((current, previous), current.astype(jnp.bfloat16))
    start = jnp.zeros((L, CYCLES), jnp.float32)
    final_state, stacked_rows = lax.scan(advance, (start, start), jnp.arange(L, dtype=jnp.float32))
    return jnp.transpose(stacked_rows, (1, 0, 2))


def with_ends(values, key, low, high):
    longest = values.shape.index(max(values.shape))
    spots = []
    for shift in (0, 1):
        where = [jax.random.randint(jax.random.fold_in(key, axis), (), 0, length) for axis, length in enumerate(values.shape)]
        where[longest] = (where[longest] + shift) % values.shape[longest]
        spots.append(tuple(where))
    return values.at[spots[0]].set(low).at[spots[1]].set(high)


def steps_of(rng, dims, shards, smallest, top_value):
    factor_of = 1.0
    for dim, shards_of in shards:
        steps = jax.random.uniform(jax.random.fold_in(jax.random.fold_in(rng, 6), dim), (shards_of,), jnp.float32, smallest / len(shards), top_value / len(shards))
        factor_of = factor_of * jnp.repeat(jnp.exp(steps), dims[dim] // shards_of).reshape((-1,) + (1,) * (len(dims) - 1 - dim))
    return factor_of


def scatter_about(stream_key, shape, deviation, most, cuts=(), kind=jnp.bfloat16):
    drawn = deviation * jax.random.normal(stream_key, shape, jnp.float32)
    if cuts:
        drawn = drawn * steps_of(stream_key, shape, cuts, -0.22, 0.18)
    return jnp.clip(drawn, -most, most).astype(kind)


def setup_inputs(seed: int = 0) -> dict:
    splits = jax.random.split(jax.random.key(seed), 7)
    sim_alm = scatter_about(splits[0], (L, NSIM, 2, L), 1.0, 6.0, ((0, 8), (1, 4)))
    t_filter = jnp.clip(jnp.exp(jax.random.uniform(splits[1], (L,), jnp.float32, math.log(0.0006510417), math.log(0.00390625))), 0.0006510417, 0.00390625)
    wiener_filter = jnp.clip(jnp.exp(jax.random.uniform(splits[2], (L,), jnp.float32, math.log(8.477105097881577e-07), math.log(5.086263172415784e-06))), 8.477105097881577e-07, 5.086263172415784e-06)
    colatitude = draw_colatitude(jax.random.fold_in(splits[6], 71), 0)
    legendre = draw_legendre(jax.random.fold_in(splits[6], 71), 0)
    pixel_mask = with_ends((jax.random.randint(splits[5], (CYCLES, NPHI), 0, 5) < 4).astype(jnp.int32), jax.random.fold_in(splits[5], 1), 0, 1)
    return {"sim_alm": sim_alm, "t_filter": t_filter, "wiener_filter": wiener_filter, "colatitude": colatitude, "legendre": legendre, "pixel_mask": pixel_mask}


def ladder(degree, orders):
    numerator = (2.0 * degree + 1.0) * (degree * degree - orders * orders)
    denominator = jnp.maximum(2.0 * degree - 1.0, 1.0)
    return jnp.where(degree > orders, jnp.sqrt(jnp.maximum(numerator, 0.0) / denominator), 0.0)

def fourier_table(mode_count, pixels):
    mode_ids = jnp.arange(mode_count, dtype=jnp.int32)[:, None]
    pixel_ids = jnp.arange(pixels, dtype=jnp.int32)[None, :]
    phases = 2.0 * math.pi / pixels * (mode_ids * pixel_ids % pixels).astype(jnp.float32)
    return jnp.stack([jnp.cos(phases).astype(jnp.bfloat16), (-jnp.sin(phases)).astype(jnp.bfloat16)], axis=1)

def reference(sim_alm, t_filter, wiener_filter, colatitude, legendre, pixel_mask):
    highest = lax.Precision.HIGHEST
    degree = jnp.arange(L, dtype=jnp.float32)
    orders = jnp.arange(L, dtype=jnp.float32)
    ladder_steps = ladder(degree[None, :], orders[:, None])
    lookup = legendre.astype(jnp.float32)
    fourier = fourier_table(L, NPHI).astype(jnp.float32)
    mode_weight = jnp.where(orders > 0, 2.0, 1.0)
    mode_weight_half = mode_weight.astype(jnp.bfloat16)
    cotangent = jnp.cos(colatitude) / jnp.sin(colatitude)
    cosecant = 1.0 / jnp.sin(colatitude)
    tilt_factor = jnp.cos(colatitude)
    pixel_weight = pixel_mask.astype(jnp.float32)

    def one_sim(coefficients):
        values = coefficients.astype(jnp.float32)
        weighted = wiener_filter * values
        raised = ladder_steps[:, None, :] * weighted
        lowered = jnp.concatenate([raised[..., 1:], jnp.zeros_like(raised[..., :1])], axis=-1)
        coefs = jnp.stack([t_filter * values, weighted, degree * weighted, lowered], axis=1).astype(jnp.bfloat16)
        legsum = jnp.einsum('mkcl,mlr->mkcr', coefs.astype(jnp.float32), lookup, precision=highest)
        rotated = jnp.stack([-legsum[:, 1, 1], legsum[:, 1, 0]], axis=1) * (orders[:, None, None] * cosecant)
        slopes = cotangent * legsum[:, 2] - cosecant * legsum[:, 3]
        cycle_coefs = jnp.stack([legsum[:, 0], rotated, slopes], axis=1).astype(jnp.bfloat16)
        scaled = cycle_coefs * mode_weight_half[:, None, None, None]
        cycle_maps = jnp.einsum('mqcr,mcj->qrj', scaled.astype(jnp.float32), fourier, precision=highest)
        product = pixel_weight * cycle_maps[0]
        flow_maps = jnp.stack([product * cycle_maps[2], product * cycle_maps[1]]).astype(jnp.bfloat16)
        mode_coefs = (jnp.einsum('prj,mcj->mpcr', flow_maps.astype(jnp.float32), fourier, precision=highest) * (2.0 * math.pi / NPHI)).astype(jnp.bfloat16)
        tilted = (tilt_factor * mode_coefs[:, 0].astype(jnp.float32)).astype(jnp.bfloat16)
        stacked = jnp.stack([tilted, mode_coefs[:, 0], mode_coefs[:, 1]], axis=1)
        projected = jnp.einsum('mkcr,mlr->mkcl', stacked.astype(jnp.float32), lookup, precision=highest)
        shifted = jnp.concatenate([jnp.zeros_like(projected[:, 1, :, :1]), projected[:, 1, :, :-1]], axis=-1)
        real_part = degree * projected[:, 0, 0] - ladder_steps * shifted[:, 0] + orders[:, None] * projected[:, 2, 1]
        imag_part = degree * projected[:, 0, 1] - ladder_steps * shifted[:, 1] - orders[:, None] * projected[:, 2, 0]
        return jnp.stack([real_part, imag_part], axis=1) / L
    estimates = lax.map(one_sim, jnp.moveaxis(sim_alm, 1, 0))
    field_sum = lax.optimization_barrier(jnp.sum(estimates, axis=0))
    residual = estimates - field_sum / NSIM
    partner = residual.reshape(NSIM // 2, 2, L, 2, L)[:, ::-1].reshape(residual.shape)
    auto_power = lax.optimization_barrier(jnp.sum(residual * residual, axis=2))
    cross_power = lax.optimization_barrier(jnp.sum(residual * partner, axis=2))
    spectra = jnp.stack([jnp.einsum('m,sml->sl', mode_weight, auto_power, precision=highest), jnp.einsum('m,sml->sl', mode_weight, cross_power, precision=highest)], axis=1)
    spectra = spectra / (2.0 * degree + 1.0)
    return (field_sum, spectra)
```

```python
import functools
import math

import jax
import jax.numpy as jnp
from jax import lax
from jax.experimental import pallas as pl
from jax.experimental.pallas import tpu as pltpu
from jax.sharding import PartitionSpec as P

F32 = jnp.float32
BF16 = jnp.bfloat16
VMEM_LIMIT = 56 * 1024 * 1024


def ladder(degree, orders):
    numerator = (2.0 * degree + 1.0) * (degree * degree - orders * orders)
    denominator = jnp.maximum(2.0 * degree - 1.0, 1.0)
    return jnp.where(degree > orders, jnp.sqrt(jnp.maximum(numerator, 0.0) / denominator), 0.0)


def divisor(total, most, multiple):
    best = None
    for size in range(multiple, most + 1, multiple):
        if total % size == 0:
            best = size
    return best if best is not None else total


def trig(phase_index, period):
    k = phase_index % period
    k = jnp.where(k >= period // 2, k - period, k)
    half = k.astype(F32) * (math.pi / period)
    square = half * half

    def series(first):
        total = jnp.zeros_like(square)
        for n in reversed(range(8)):
            total = total * square + (-1.0) ** n / math.factorial(2 * n + first)
        return total

    sine = half * series(1)
    cosine = series(0)
    return 1.0 - 2.0 * sine * sine, 2.0 * sine * cosine


def legsum_kernel(alm_ref, t_ref, w_ref, leg_ref, angle_ref, first_ref, out_ref):
    block, rows, degrees = alm_ref.shape
    degree = lax.broadcasted_iota(jnp.int32, (1, degrees), 1).astype(F32)
    first = first_ref[0] + pl.program_id(0) * block
    t_filter = t_ref[...]
    w_filter = w_ref[...]
    cotangent = angle_ref[0:1, :]
    cosecant = angle_ref[1:2, :]
    parity = lax.broadcasted_iota(jnp.int32, (rows, leg_ref.shape[1]), 0) % 2
    for i in range(block):
        order = (first + i).astype(F32)
        steps = ladder(degree, order)
        values = alm_ref[i].astype(F32)
        weighted = w_filter * values
        raised = steps * weighted
        lowered = jnp.where(degree < degrees - 1, pltpu.roll(raised, degrees - 1, 1), 0.0)
        coefs = jnp.concatenate(
            [t_filter * values, weighted, degree * weighted, lowered], axis=0
        ).astype(BF16)
        sums = lax.dot_general(
            coefs, leg_ref[i], (((1,), (1,)), ((), ())), preferred_element_type=F32
        )
        wave = sums[rows : 2 * rows]
        rotated = jnp.where(
            parity == 0, -pltpu.roll(wave, rows - 1, 0), pltpu.roll(wave, 1, 0)
        ) * (cosecant * order)
        slopes = cotangent * sums[2 * rows : 3 * rows] - cosecant * sums[3 * rows :]
        out_ref[i] = jnp.concatenate([sums[:rows], rotated, slopes], axis=0)


def maps_kernel(x_ref, mask_ref, fine_ref, coarse_ref, out_ref, table, total, *, modes, scale):
    step = pl.program_id(0)
    fine = fine_ref.shape[1]
    coarse = coarse_ref.shape[1]
    rows = mask_ref.shape[0]
    fine_cos = fine_ref[0]
    fine_sin = fine_ref[1]
    for a in range(coarse):
        cos_a = coarse_ref[0, a : a + 1, :]
        sin_a = coarse_ref[1, a : a + 1, :]
        table[a * fine : (a + 1) * fine, :] = (fine_cos * cos_a - fine_sin * sin_a).astype(BF16)
        table[modes + a * fine : modes + (a + 1) * fine, :] = (
            -(fine_sin * cos_a + fine_cos * sin_a)
        ).astype(BF16)
    maps = jnp.dot(x_ref[...], table[...], preferred_element_type=F32)
    product = mask_ref[...] * maps[:rows]
    flows = jnp.concatenate(
        [product * maps[2 * rows :], product * maps[rows : 2 * rows]], axis=0
    ).astype(BF16)
    part = lax.dot_general(
        flows, table[...], (((1,), (1,)), ((), ())), preferred_element_type=F32
    )

    @pl.when(step == 0)
    def _():
        total[...] = part

    @pl.when(step > 0)
    def _():
        total[...] += part

    @pl.when(step == pl.num_programs(0) - 1)
    def _():
        out_ref[...] = (total[...] * scale).astype(BF16)


def project_kernel(x_ref, leg_ref, first_ref, field_ref, auto_ref, cross_ref):
    block = x_ref.shape[0]
    degrees = leg_ref.shape[2]
    rows = auto_ref.shape[0]
    degree = lax.broadcasted_iota(jnp.int32, (1, degrees), 1).astype(F32)
    first = first_ref[0] + pl.program_id(0) * block
    auto = jnp.zeros((rows, degrees), F32)
    cross = jnp.zeros((rows, degrees), F32)
    inverse = 1.0 / degrees

    def combine(one, two, three, steps, order):
        shifted = jnp.where(degree > 0, pltpu.roll(two, 1, 1), 0.0)
        return (degree * one - steps * shifted + order * three) * inverse

    for i in range(block):
        order = (first + i).astype(F32)
        steps = ladder(degree, order)
        leg = leg_ref[i]
        both = jnp.concatenate([leg, leg], axis=0)
        sums = jnp.dot(x_ref[i], both, preferred_element_type=F32)
        residual = combine(
            sums[:rows], sums[rows : 2 * rows], sums[2 * rows : 3 * rows], steps, order
        )
        base = 3 * rows
        field = combine(
            sums[base : base + 2], sums[base + 2 : base + 4], sums[base + 4 : base + 6], steps, order
        )
        field_ref[i] = field
        weight = jnp.where(order > 0, 2.0, 1.0)
        weighted = weight * residual
        auto = auto + weighted * residual
        cross = cross + weighted * pltpu.roll(residual, rows - 2, 0)

    @pl.when(pl.program_id(0) == 0)
    def _():
        auto_ref[...] = auto
        cross_ref[...] = cross

    @pl.when(pl.program_id(0) > 0)
    def _():
        auto_ref[...] += auto
        cross_ref[...] += cross


def params():
    return pltpu.CompilerParams(
        dimension_semantics=("arbitrary",), vmem_limit_bytes=VMEM_LIMIT
    )


def per_device(sim_alm, t_filter, wiener_filter, colatitude, legendre, pixel_mask):
    local_modes, sims_here, _, degrees = sim_alm.shape
    cycle_count = legendre.shape[2]
    pixels = pixel_mask.shape[1]
    blocks = lax.axis_size("blk")
    cycle_local = cycle_count // blocks
    modes = degrees
    first_mode = (lax.axis_index("blk") * local_modes).astype(jnp.int32).reshape(1)
    degree = jnp.arange(degrees, dtype=F32)
    rows = 2 * sims_here
    smem = pl.BlockSpec(memory_space=pltpu.SMEM)

    angles = jnp.stack([jnp.cos(colatitude) / jnp.sin(colatitude), 1.0 / jnp.sin(colatitude)])
    leg_rows = jnp.transpose(legendre, (0, 2, 1))
    block = divisor(local_modes, 8, 1)
    cycle_coefs = pl.pallas_call(
        legsum_kernel,
        grid=(local_modes // block,),
        in_specs=[
            pl.BlockSpec((block, rows, degrees), lambda i: (i, 0, 0)),
            pl.BlockSpec((1, degrees), lambda i: (0, 0)),
            pl.BlockSpec((1, degrees), lambda i: (0, 0)),
            pl.BlockSpec((block, cycle_count, degrees), lambda i: (i, 0, 0)),
            pl.BlockSpec((2, cycle_count), lambda i: (0, 0)),
            smem,
        ],
        out_specs=pl.BlockSpec((block, 3 * rows, cycle_count), lambda i: (i, 0, 0)),
        out_shape=jax.ShapeDtypeStruct((local_modes, 3 * rows, cycle_count), F32),
        compiler_params=params(),
        name="legsum",
    )(
        sim_alm.reshape(local_modes, rows, degrees),
        t_filter[None],
        wiener_filter[None],
        leg_rows,
        angles,
        first_mode,
    )

    sent = cycle_coefs.astype(BF16).reshape(local_modes, 3 * rows, blocks, cycle_local)
    sent = jnp.transpose(sent, (2, 1, 3, 0)).reshape(blocks, 3 * rows * cycle_local, local_modes)
    arrived = lax.all_to_all(sent, "blk", split_axis=0, concat_axis=0, tiled=True)
    arrived = arrived.reshape(blocks, 3 * sims_here, 2, cycle_local, local_modes)
    arrived = jnp.transpose(arrived, (1, 3, 2, 0, 4)).reshape(
        3 * sims_here * cycle_local, 2, modes
    )
    mode_weight = jnp.where(jnp.arange(modes) > 0, 2.0, 1.0).astype(BF16)
    scaled = (arrived * mode_weight).reshape(3 * sims_here * cycle_local, 2 * modes)

    map_rows = sims_here * cycle_local
    fine = divisor(modes, 64, 8)
    coarse = modes // fine
    pixel_ids = jnp.arange(pixels, dtype=jnp.int32)[None, :]
    fine_table = jnp.stack(trig(jnp.arange(fine, dtype=jnp.int32)[:, None] * pixel_ids, pixels))
    coarse_table = jnp.stack(
        trig(jnp.arange(coarse, dtype=jnp.int32)[:, None] * fine * pixel_ids, pixels)
    )
    mask_rows = jnp.tile(pixel_mask.astype(F32), (sims_here, 1))
    span = divisor(pixels, 512, 128)
    mode_coefs = pl.pallas_call(
        functools.partial(maps_kernel, modes=modes, scale=2.0 * math.pi / pixels),
        grid=(pixels // span,),
        in_specs=[
            pl.BlockSpec((3 * map_rows, 2 * modes), lambda j: (0, 0)),
            pl.BlockSpec((map_rows, span), lambda j: (0, j)),
            pl.BlockSpec((2, fine, span), lambda j: (0, 0, j)),
            pl.BlockSpec((2, coarse, span), lambda j: (0, 0, j)),
        ],
        out_specs=pl.BlockSpec((2 * map_rows, 2 * modes), lambda j: (0, 0)),
        out_shape=jax.ShapeDtypeStruct((2 * map_rows, 2 * modes), BF16),
        scratch_shapes=[
            pltpu.VMEM((2 * modes, span), BF16),
            pltpu.VMEM((2 * map_rows, 2 * modes), F32),
        ],
        compiler_params=params(),
        name="maps",
    )(scaled, mask_rows, fine_table, coarse_table)

    back = mode_coefs.reshape(2, sims_here, cycle_local, 2, blocks, local_modes)
    back = jnp.transpose(back, (4, 0, 1, 3, 2, 5)).reshape(
        blocks, 2 * rows * cycle_local, local_modes
    )
    returned = lax.all_to_all(back, "blk", split_axis=0, concat_axis=0, tiled=True)
    returned = returned.reshape(blocks, 2, sims_here, 2, cycle_local, local_modes)
    returned = jnp.transpose(returned, (5, 1, 2, 3, 0, 4)).reshape(
        local_modes, 2, sims_here, 2, cycle_count
    )
    first_flow = returned[:, 0].astype(F32)
    second_flow = returned[:, 1].astype(F32)
    tilted = (jnp.cos(colatitude) * first_flow).astype(BF16).astype(F32)
    turned = jnp.stack([second_flow[:, :, 1], -second_flow[:, :, 0]], axis=2)
    stacked = jnp.stack([tilted, first_flow, turned], axis=1)
    field_coefs = lax.psum(jnp.sum(stacked, axis=2), "sims")
    sim_total = sims_here * lax.axis_size("sims")
    centred = (stacked - field_coefs[:, :, None] / sim_total).reshape(
        local_modes, 3 * rows, cycle_count
    )
    spare = (-(3 * rows + 6)) % 8
    lines = jnp.concatenate(
        [
            centred,
            field_coefs.reshape(local_modes, 6, cycle_count),
            jnp.zeros((local_modes, spare, cycle_count), F32),
        ],
        axis=1,
    )
    upper = lax.reduce_precision(lines, 8, 7)
    lines = jnp.concatenate([upper.astype(BF16), (lines - upper).astype(BF16)], axis=2)

    height = lines.shape[1]
    field_total, auto, cross = pl.pallas_call(
        project_kernel,
        grid=(local_modes // block,),
        in_specs=[
            pl.BlockSpec((block, height, 2 * cycle_count), lambda i: (i, 0, 0)),
            pl.BlockSpec((block, cycle_count, degrees), lambda i: (i, 0, 0)),
            smem,
        ],
        out_specs=[
            pl.BlockSpec((block, 2, degrees), lambda i: (i, 0, 0)),
            pl.BlockSpec((rows, degrees), lambda i: (0, 0)),
            pl.BlockSpec((rows, degrees), lambda i: (0, 0)),
        ],
        out_shape=[
            jax.ShapeDtypeStruct((local_modes, 2, degrees), F32),
            jax.ShapeDtypeStruct((rows, degrees), F32),
            jax.ShapeDtypeStruct((rows, degrees), F32),
        ],
        compiler_params=params(),
        name="project",
    )(lines, leg_rows, first_mode)

    quarter = degrees // lax.axis_size("sims")
    field_share = lax.dynamic_slice_in_dim(
        field_total, lax.axis_index("sims") * quarter, quarter, 2
    )
    auto_power = auto.reshape(sims_here, 2, degrees).sum(axis=1)
    pair_power = cross.reshape(sims_here // 2, 2, 2, degrees)[:, 0].sum(axis=1)
    cross_power = jnp.repeat(pair_power, 2, axis=0)
    summed = lax.psum(jnp.stack([auto_power, cross_power], axis=1), "blk")
    return (field_share, summed / (2.0 * degree + 1.0))


def solution(mesh):
    placed = (P("blk", "sims", None, None), P(), P(), P(), P("blk", None, None), P("blk", None))
    return jax.shard_map(
        per_device,
        mesh=mesh,
        in_specs=placed,
        out_specs=(P("blk", None, "sims"), P("sims", None, None)),
        check_vma=False,
    )
```
